32 devices in a mesh: expert: 16 (over z, y, core), dp: 2 (over x).
Axes of the slice: x: 2, y: 2, z: 4, core: 2. Of those that a mesh axis runs over, the one named last changes fastest.
Arguments:
- tokens: bfloat16 [4096, 2048], P(('expert', 'dp')), may hold values from -6 to 6
- cotangent: bfloat16 [4096, 2048], P(('expert', 'dp')), may hold values from -6 to 6
- routes: int32 [4096, 8], P(('expert', 'dp')), may hold values from 0 to 15, all different within a row; in each aligned block of 128 rows (0 to 127, 128 to 255, ...) at most 72 rows name the same one
- route_weight: float32 [4096, 8], P(('expert', 'dp')), may hold values from 0.05 to 1
- gate_weight: bfloat16 [16, 768, 2048], P('expert', 'dp'), may hold values from -6 to 6
- up_weight: bfloat16 [16, 768, 2048], P('expert', 'dp'), may hold values from -6 to 6
- down_weight: bfloat16 [16, 768, 2048], P('expert', 'dp'), may hold values from -6 to 6
- cluster_of: int32 [16], replicated, may hold values from 0 to 7, as said below
- owner: int32 [8], replicated, may hold values from 0 to 7, each once
Outputs:
- merged_gate: bfloat16 [16, 768, 1024], P('expert', 'dp')
- merged_up: bfloat16 [16, 768, 1024], P('expert', 'dp')
- merged_down: bfloat16 [16, 768, 1024], P('expert', 'dp')
- share: float32 [16, 768], P('expert', 'dp')
The draws below stay inside these ranges and needn't reach their ends.
Inputs may be any that keep to these rules, and one draw needn't show every extreme that they name: `routes`: at most 72 of the rows of one device name the same expert, and every expert is named by at least one row. `cluster_of`: every one of the 8 clusters has at least one member. Each owner pair owns exactly one cluster.
All inputs are finite; a program needn't handle non-finite values.
Results may differ from the reference program's by a relative error of at most 0.0014.
Values may be sent and summed in bfloat16 or wider, within the bound.
A program may use at most 128 MiB of HBM per device.

```python
import math
import jax
import jax.numpy as jnp
import numpy as np
from jax import lax

D = 2048
HID = 768
TOPK = 8
TOK_DEV = 128
EXPERTS = 16
CLUSTERS = 8
CAP = 72
TOKENS = 4096
N_EXPERT = 16
N_DP = 2


def draw_cluster_of(key, part):
    first = jnp.arange(CLUSTERS, dtype=jnp.int32)
    others = jax.random.randint(jax.random.fold_in(key, 11), (EXPERTS - CLUSTERS,), 0, CLUSTERS, dtype=jnp.int32)
    labels = jnp.concatenate([first, others])
    order = jax.random.permutation(jax.random.fold_in(key, 12), EXPERTS)
    return labels[order].astype(jnp.int32)


def block_scale(stream_key, dims, shards, smallest, largest):
    factor_of, own = 1.0, jax.random.fold_in(stream_key, 6)
    for axis_at, shards_of in shards:
        heights = jnp.exp(jax.random.uniform(jax.random.fold_in(own, axis_at), (shards_of,), jnp.float32, smallest / len(shards), largest / len(shards)))
        factor_of = factor_of * jnp.repeat(heights, dims[axis_at] // shards_of).reshape([-1 if axis == axis_at else 1 for axis in range(len(dims))])
    return factor_of


def assign_block(stream_key, own, number, rows, amount, top, most, lean):
    ranking = jax.random.permutation(stream_key, amount)
    heavy_load, usual = portions_of(amount, rows * top, most, lean, True), portions_of(amount, rows * top, most, lean, False)
    places = jnp.arange(amount)

    def named(sizes, turn):
        used = int((sizes > 0).sum())
        fixed = max(1, used // 4)
        shifted = fixed + (places - fixed + turn * (used - fixed)) % max(1, amount - fixed)
        return jnp.zeros((amount,), jnp.int32).at[ranking[jnp.where(places < fixed, places, shifted)]].set(jnp.asarray(sizes, jnp.int32))

    sizes = jnp.where(number % 4 == 0, named(heavy_load, number // 4), named(usual, number - number // 4 - 1))
    mixed = jax.random.permutation(jax.random.fold_in(own, 3), amount)
    donor, receiver = mixed[0:amount // 2 * 2:2], mixed[1:amount // 2 * 2:2]
    room = jnp.minimum(sizes[donor] - 1, most - sizes[receiver]) // 2
    room = jnp.where((donor == ranking[0]) | (receiver == ranking[0]) | (sizes[receiver] == 0), 0, jnp.maximum(room, 0))
    shifted = jax.random.randint(jax.random.fold_in(own, 4), (amount // 2,), 0, 1 << 20) % (room + 1)
    sizes = sizes.at[donor].add(-shifted).at[receiver].add(shifted)
    items = jnp.searchsorted(jnp.cumsum(sizes), jnp.arange(rows * top), side="right").astype(jnp.int32)
    grid = items.reshape(top, rows).T
    grid = grid[jax.random.permutation(jax.random.fold_in(own, 1), rows)]
    turn = jax.random.randint(jax.random.fold_in(own, 2), (rows, 1), 0, top)
    return jnp.take_along_axis(grid, (jnp.arange(top)[None, :] + turn) % top, axis=1)


def portions_of(count, total, limit, slope, full):
    loads = [(1 << 20) // math.isqrt(rank ** slope) + 1 for rank in range(1, count + 1)]
    largest = limit if full else min(limit, max(-(-total // count), total * loads[0] // sum(loads)))
    least = 1 if total - largest >= count - 1 else 0
    given, surplus = [largest] + [least] * (count - 1), total - largest - least * (count - 1)
    while surplus > 0:
        movable = [i for i in range(1, count) if given[i] < largest] or [i for i in range(1, count) if given[i] < limit]
        mass, left = sum([loads[i] for i in movable]), surplus
        for i in movable:
            more = min(limit - given[i], max(1, left * loads[i] // mass), surplus)
            given[i] = given[i] + more
            surplus = surplus - more
    return np.array(given)


def gaussian(rng, dims, deviation, most, shards=(), held_as=jnp.bfloat16):
    array = deviation * jax.random.normal(rng, dims, jnp.float32)
    if shards:
        array = array * block_scale(rng, dims, shards, -0.22, 0.18)
    return jnp.clip(array, -most, most).astype(held_as)


def setup_inputs(seed: int = 0) -> dict:
    seeds = jax.random.split(jax.random.key(seed), 10)
    tokens = gaussian(seeds[0], (TOKENS, D), 1.0, 6.0, ((0, 32),))
    cotangent = gaussian(seeds[1], (TOKENS, D), 1.0, 6.0, ((0, 32),))
    routes_keys = jax.random.split(jax.random.fold_in(seeds[2], 1), TOKENS // TOK_DEV)
    routes_turns = jax.random.permutation(jax.random.fold_in(seeds[2], 3), TOKENS // TOK_DEV)
    routes = jax.vmap(lambda own, number: assign_block(jax.random.fold_in(seeds[2], 2), own, number, TOK_DEV, EXPERTS, TOPK, CAP, 2))(routes_keys, routes_turns).reshape((TOKENS, TOPK))
    route_weight = jnp.clip(jnp.exp(math.log(1.0) - 2.9957323 * jax.random.uniform(seeds[3], (TOKENS, TOPK), jnp.float32) ** block_scale(seeds[3], (TOKENS, TOPK), ((0, 32),), -0.2, 0.2)), 0.05, 1.0)
    gate_weight = gaussian(seeds[4], (EXPERTS, HID, D), 1.0, 6.0, ((0, 16), (1, 2)))
    up_weight = gaussian(seeds[5], (EXPERTS, HID, D), 1.0, 6.0, ((0, 16), (1, 2)))
    down_weight = gaussian(seeds[6], (EXPERTS, HID, D), 1.0, 6.0, ((0, 16), (1, 2)))
    cluster_of = draw_cluster_of(jax.random.fold_in(seeds[9], 71), 0)
    owner = jax.random.permutation(seeds[8], CLUSTERS).astype(jnp.int32)
    return dict(tokens=tokens, cotangent=cotangent, routes=routes, route_weight=route_weight, gate_weight=gate_weight, up_weight=up_weight, down_weight=down_weight, cluster_of=cluster_of, owner=owner)


def reference(tokens, cotangent, routes, route_weight, gate_weight, up_weight, down_weight, cluster_of, owner):
    energy = lax.optimization_barrier(jnp.mean(jnp.square(cotangent.astype(jnp.float32)), axis=1))
    scales = (jnp.square(route_weight) * energy[:, None]).astype(jnp.bfloat16).astype(jnp.float32).reshape(-1)
    flat_ids = routes.reshape(-1).astype(jnp.int32)
    order = jnp.argsort(flat_ids, stable=True).astype(jnp.int32)
    counts = jnp.bincount(flat_ids, length=EXPERTS).astype(jnp.int32)
    starts = (jnp.cumsum(counts) - counts).astype(jnp.int32)
    most_rows = N_EXPERT * N_DP * CAP
    padded = jnp.concatenate([order, jnp.zeros((most_rows,), jnp.int32)])
    factor = 1.0 / jnp.sqrt(jnp.float32(D))

    def fisher_one(expert_id):
        index_rows = lax.dynamic_slice(padded, (starts[expert_id],), (most_rows,))
        valid = jnp.arange(most_rows, dtype=jnp.int32) < counts[expert_id]
        inputs = tokens[index_rows // TOPK]
        weights_s = jnp.where(valid, scales[index_rows], jnp.float32(0.0))
        pre_gate = jnp.dot(inputs, gate_weight[expert_id].T, preferred_element_type=jnp.float32) * factor
        pre_up = jnp.dot(inputs, up_weight[expert_id].T, preferred_element_type=jnp.float32) * factor
        act = jax.nn.silu(pre_gate) * pre_up
        return jnp.dot(weights_s, act * act, precision=lax.Precision.HIGHEST)
    fisher = lax.map(fisher_one, jnp.arange(EXPERTS, dtype=jnp.int32))
    members = (cluster_of[None, :] == jnp.arange(CLUSTERS, dtype=jnp.int32)[:, None]).astype(jnp.float32)
    totals = jnp.dot(members, fisher, precision=lax.Precision.HIGHEST)
    share = fisher / totals[cluster_of]
    inverse = jnp.argsort(owner).astype(jnp.int32)

    def merge_all(weight):

        def one_cluster(cluster_row):
            weighted = weight.astype(jnp.float32) * share[:, :, None]
            return jnp.einsum('e,ejd->jd', cluster_row, weighted, precision=lax.Precision.HIGHEST).astype(jnp.bfloat16)
        merged = lax.map(one_cluster, members)
        by_owner = merged[inverse]
        return by_owner.reshape(CLUSTERS, HID, 2, D // 2).transpose(0, 2, 1, 3).reshape(EXPERTS, HID, D // 2)
    return (merge_all(gate_weight), merge_all(up_weight), merge_all(down_weight), share)
```

```python
import functools

import jax
import jax.numpy as jnp
from jax import lax
from jax.experimental import pallas as pl
from jax.experimental.pallas import tpu as pltpu
from jax.sharding import PartitionSpec as P

LANES = 128
MESH = pl.DeviceIdType.MESH


def spread_kernel(
    tokens_ref, gate_ref, up_ref, down_ref, got_ref, fisher_ref,
    rows_ref, held_ref, parts_ref, others_ref, block_ref,
    token_send, token_recv, piece_send, piece_recv, swap_send, swap_recv,
    part_send, part_recv, share_send, share_recv, local_sem,
    *, factor,
):
    experts, dp_count = lax.axis_size("expert"), lax.axis_size("dp")
    depth = experts // 4
    me, my_dp = lax.axis_index("expert"), lax.axis_index("dp")
    z, y, core = me // 4, (me // 2) % 2, me % 2
    row_count = tokens_ref.shape[0]
    model_width = gate_ref.shape[1]
    half_cols = model_width // 2
    piece_rows = got_ref.shape[2]
    weights = (gate_ref, up_ref, down_ref)
    far_side, near_side = (1 - z // (depth // 2)) * (depth // 2), z // (depth // 2) * (depth // 2)
    peers = [
        (far_side + (z + dz) % (depth // 2)) * 4 + (me + k) % 4 for k in (0, 2, 1, 3) for dz in range(depth // 2)
    ] + [
        (near_side + (z + dz) % (depth // 2)) * 4 + (me + k) % 4 for dz in range(1, depth // 2) for k in (0, 2, 1, 3)
    ] + [z * 4 + (me + k) % 4 for k in (2, 1, 3)]
    dp_of = [(my_dp + k) % dp_count for k in range(dp_count)]

    barrier = pltpu.get_barrier_semaphore()
    for peer in peers:
        pl.semaphore_signal(barrier, inc=1, device_id={"expert": peer}, device_id_type=MESH)
    for other in dp_of[1:]:
        pl.semaphore_signal(barrier, inc=1, device_id={"dp": other}, device_id_type=MESH)
    own = [
        pltpu.make_async_copy(tokens_ref, rows_ref.at[me], local_sem.at[0]),
        pltpu.make_async_copy(gate_ref, held_ref.at[0, 0], local_sem.at[1]),
        pltpu.make_async_copy(up_ref, held_ref.at[0, 1], local_sem.at[2]),
        pltpu.make_async_copy(
            down_ref.at[pl.ds((me // 2) * piece_rows, piece_rows), pl.ds((me % 2) * half_cols, half_cols)],
            block_ref, local_sem.at[3],
        ),
    ]
    for copy in own:
        copy.start()
    pl.semaphore_wait(barrier, experts - 1 + dp_count - 1)

    def token_copy(slot, kind, peer, source=None):
        return pltpu.make_async_remote_copy(
            src_ref=rows_ref.at[slot] if source is None else source,
            dst_ref=rows_ref.at[slot],
            send_sem=token_send.at[kind, slot],
            recv_sem=token_recv.at[slot],
            device_id={"expert": peer},
            device_id_type=MESH,
        )

    across = z * 4 + (1 - y) * 2 + core
    partner = z * 4 + y * 2 + (1 - core)

    def own_line(act):
        source = tokens_ref
        for sign, kind in ((1, 0), (-1, 1)):
            @pl.when((z + sign >= 0) & (z + sign < depth))
            def _():
                act(token_copy(me, kind, me + 4 * sign, source), None)
        act(token_copy(me, 2, across, source), None)
        act(token_copy(me, 3, partner, source), None)

    def line(act):
        for distance in range(1, depth):
            for sign, kind in ((1, 0), (-1, 1)):
                origin = z - sign * distance

                @pl.when((origin >= 0) & (origin < depth))
                def _():
                    slot = origin * 4 + y * 2 + core
                    act(None, slot)

                    @pl.when((z + sign >= 0) & (z + sign < depth))
                    def _():
                        act(token_copy(slot, kind, me + 4 * sign), None)
                    act(token_copy(slot, 2, across), None)
                    act(token_copy(slot, 3, partner), None)

    def beside(act):
        for distance in range(depth):
            for sign in (1, -1) if distance else (1,):
                origin = z - sign * distance

                @pl.when((origin >= 0) & (origin < depth))
                def _():
                    slot = origin * 4 + (1 - y) * 2 + core
                    act(None, slot)
                    act(token_copy(slot, 3, partner), None)

    def begin(copy, slot):
        if copy is None:
            token_copy(slot, 0, partner).wait_recv()
        else:
            copy.start()

    def finish(copy, slot):
        if copy is not None:
            copy.wait_send()

    def piece_copy(which, peer, landing):
        return pltpu.make_async_remote_copy(
            src_ref=weights[which].at[
                pl.ds((peer // 2) * piece_rows, piece_rows), pl.ds((peer % 2) * half_cols, half_cols)
            ],
            dst_ref=got_ref.at[landing, which],
            send_sem=piece_send.at[peer, which],
            recv_sem=piece_recv.at[landing, which],
            device_id={"expert": peer},
            device_id_type=MESH,
        )

    def swap_copy(shift, which):
        return pltpu.make_async_remote_copy(
            src_ref=weights[which],
            dst_ref=held_ref.at[shift, which],
            send_sem=swap_send.at[shift, which],
            recv_sem=swap_recv.at[shift, which],
            device_id={"dp": dp_of[(dp_count - shift) % dp_count]},
            device_id_type=MESH,
        )

    swaps = [swap_copy(shift, which) for shift in range(1, dp_count) for which in range(2)]
    for copy in swaps:
        copy.start()
    own_line(begin)
    for peer in peers:
        piece_copy(0, peer, me).start()
    line(begin)
    for peer in peers:
        for which in range(1, 3):
            piece_copy(which, peer, me).start()
    for copy in own:
        copy.wait()
    keep = [
        pltpu.make_async_copy(
            held_ref.at[0, which, pl.ds((me // 2) * piece_rows, piece_rows), pl.ds((me % 2) * half_cols, half_cols)],
            got_ref.at[me, which], local_sem.at[which],
        )
        for which in range(2)
    ] + [pltpu.make_async_copy(block_ref, got_ref.at[me, 2], local_sem.at[2])]
    for copy in keep:
        copy.start()
    beside(begin)
    for zs in range(depth):
        for ys in range(2):
            token_copy(zs * 4 + ys * 2 + 1 - core, 0, partner).wait_recv()

    contract = (((1,), (1,)), ((), ()))
    group = 4 if experts % 4 == 0 else 1
    for shift in range(dp_count):
        if shift:
            for which in range(2):
                swap_copy(shift, which).wait_recv()
        parts_ref[shift] = jnp.zeros_like(parts_ref[shift])

        def step(index, carry):
            block = rows_ref[pl.ds(index * group, group)].reshape(group * row_count, rows_ref.shape[2])
            tokens = block[:, :model_width]
            pre_gate = lax.dot_general(
                tokens, held_ref[shift, 0], contract, preferred_element_type=jnp.float32) * factor
            pre_up = lax.dot_general(
                tokens, held_ref[shift, 1], contract, preferred_element_type=jnp.float32) * factor
            act = pre_gate / (1.0 + jnp.exp(-pre_gate)) * pre_up
            columns = block[:, model_width:].astype(jnp.float32)
            lane = lax.broadcasted_iota(jnp.int32, columns.shape, 1)
            scale = jnp.sum(jnp.where(lane == me, columns, 0.0), axis=1, keepdims=True)
            parts_ref[shift] += jnp.sum(act * act * scale, axis=0, keepdims=True)
            return carry

        lax.fori_loop(0, experts // group, step, 0)

    def part_copy(shift):
        return pltpu.make_async_remote_copy(
            src_ref=parts_ref.at[shift],
            dst_ref=others_ref.at[shift],
            send_sem=part_send.at[shift],
            recv_sem=part_recv.at[shift],
            device_id={"dp": dp_of[shift]},
            device_id_type=MESH,
        )

    for shift in range(1, dp_count):
        part_copy(shift).start()
    total = parts_ref[0]
    for shift in range(1, dp_count):
        part_copy(shift).wait()
        total = total + others_ref[shift]
    fisher_ref[me] = total

    def share_copy(peer, landing):
        return pltpu.make_async_remote_copy(
            src_ref=fisher_ref.at[me],
            dst_ref=fisher_ref.at[landing],
            send_sem=share_send.at[peer],
            recv_sem=share_recv.at[landing],
            device_id={"expert": peer},
            device_id_type=MESH,
        )

    for peer in peers:
        share_copy(peer, me).start()
    own_line(finish)
    line(finish)
    beside(finish)
    for copy in swaps:
        copy.wait_send()
    for copy in keep:
        copy.wait()
    for peer in peers:
        share_copy(peer, me).wait_send()
        pltpu.make_async_remote_copy(
            src_ref=fisher_ref.at[me], dst_ref=fisher_ref.at[peer], send_sem=share_send.at[peer],
            recv_sem=share_recv.at[peer], device_id={"expert": peer}, device_id_type=MESH,
        ).wait_recv()
        for which in range(3):
            piece_copy(which, peer, me).wait_send()
            piece_copy(which, peer, peer).wait_recv()


def spread(extended, gate, up, down):
    experts, dp_count = lax.axis_size("expert"), lax.axis_size("dp")
    row_count, wide = extended.shape
    hid_dev, model_width = gate.shape
    piece_rows, half_cols = hid_dev // (experts // 2), model_width // 2
    anywhere = pl.BlockSpec(memory_space=pl.ANY)
    dma = pltpu.SemaphoreType.DMA
    got, fisher = pl.pallas_call(
        functools.partial(spread_kernel, factor=1.0 / float(model_width) ** 0.5),
        out_shape=(
            jax.ShapeDtypeStruct((experts, 3, piece_rows, half_cols), jnp.bfloat16),
            jax.ShapeDtypeStruct((experts, 1, hid_dev), jnp.float32),
        ),
        in_specs=[anywhere] * 4,
        out_specs=(anywhere, pl.BlockSpec(memory_space=pltpu.VMEM)),
        scratch_shapes=[
            pltpu.VMEM((experts, row_count, wide), jnp.bfloat16),
            pltpu.VMEM((dp_count, 2, hid_dev, model_width), jnp.bfloat16),
            pltpu.VMEM((dp_count, 1, hid_dev), jnp.float32),
            pltpu.VMEM((dp_count, 1, hid_dev), jnp.float32),
            pltpu.VMEM((piece_rows, half_cols), jnp.bfloat16),
            dma((4, experts)), dma((experts,)),
            dma((experts, 3)), dma((experts, 3)),
            dma((dp_count, 2)), dma((dp_count, 2)),
            dma((dp_count,)), dma((dp_count,)),
            dma((experts,)), dma((experts,)),
            dma((4,)),
        ],
        compiler_params=pltpu.CompilerParams(
            collective_id=0, has_side_effects=True, vmem_limit_bytes=60 * 1024 * 1024
        ),
        name="spread",
    )(extended, gate, up, down)
    return got.reshape(experts, 3 * piece_rows, half_cols), fisher[:, 0, :]


def merge_kernel(place_ref, share_ref, got_ref, out_ref, total_ref):
    total_ref[...] = jnp.zeros_like(total_ref)

    def add(expert, carry):
        place = place_ref[expert]
        weighted = got_ref[expert].astype(jnp.float32) * share_ref[expert]
        total_ref[place] = total_ref[place] + weighted
        return carry

    lax.fori_loop(0, got_ref.shape[0], add, 0)
    out_ref[...] = total_ref[...].astype(jnp.bfloat16)


def merge_blocks(place, share, got, clusters):
    shape = (clusters,) + got.shape[1:]
    return pl.pallas_call(
        merge_kernel,
        out_shape=jax.ShapeDtypeStruct(shape, jnp.bfloat16),
        in_specs=[
            pl.BlockSpec(memory_space=pltpu.SMEM),
            pl.BlockSpec(memory_space=pltpu.VMEM),
            pl.BlockSpec(memory_space=pltpu.VMEM),
        ],
        out_specs=pl.BlockSpec(memory_space=pltpu.VMEM),
        scratch_shapes=[pltpu.VMEM(shape, jnp.float32)],
        cost_estimate=pl.CostEstimate(flops=2 * got.size, bytes_accessed=3 * got.size, transcendentals=0),
        name="merge",
    )(place, share, got)


def routed_fisher(tokens, scales, routes, gate_weight, up_weight, capacity):
    expert_count = lax.axis_size("expert")
    row_count, model_width = tokens.shape
    top_count = routes.shape[1]
    scales = scales.reshape(-1)
    flat_ids = routes.reshape(-1)
    one_hot = (flat_ids[:, None] == jnp.arange(expert_count, dtype=jnp.int32)[None, :]).astype(
        jnp.int32
    )
    rank_ids = jnp.sum((jnp.cumsum(one_hot, axis=0) - one_hot) * one_hot, axis=1)
    slot_ids = flat_ids * capacity + rank_ids
    source = jnp.arange(row_count * top_count, dtype=jnp.int32) // top_count
    send_rows = (
        jnp.zeros((expert_count * capacity, model_width), jnp.bfloat16)
        .at[slot_ids]
        .set(tokens[source])
    )
    send_scales = jnp.zeros((expert_count * capacity,), jnp.bfloat16).at[slot_ids].set(scales)
    recv_rows, recv_scales = (
        lax.all_to_all(
            send_rows.reshape(expert_count, capacity, model_width),
            "expert",
            split_axis=0,
            concat_axis=0,
            tiled=True,
        ),
        lax.all_to_all(
            send_scales.reshape(expert_count, capacity),
            "expert",
            split_axis=0,
            concat_axis=0,
            tiled=True,
        ),
    )
    inputs = recv_rows.reshape(-1, model_width)
    weights_s = recv_scales.reshape(-1).astype(jnp.float32)
    hid_dev = gate_weight.shape[1]
    factor = 1.0 / jnp.sqrt(jnp.float32(model_width))
    pre_gate = (
        jnp.dot(
            inputs,
            lax.all_gather(gate_weight[0], "dp", axis=0, tiled=True).T,
            preferred_element_type=jnp.float32,
        )
        * factor
    )
    pre_up = (
        jnp.dot(
            inputs,
            lax.all_gather(up_weight[0], "dp", axis=0, tiled=True).T,
            preferred_element_type=jnp.float32,
        )
        * factor
    )
    act = jax.nn.silu(pre_gate) * pre_up
    part = jnp.dot(weights_s, act * act, precision=lax.Precision.HIGHEST)
    whole_sum = lax.psum(part, "dp")
    own_fisher = lax.dynamic_slice_in_dim(whole_sum, lax.axis_index("dp") * hid_dev, hid_dev)
    return lax.all_gather(own_fisher[None, :], "expert", axis=0, tiled=True)


def deliver_kernel(
    place_ref, share_ref, got_ref, gate_ref, up_ref, down_ref, merged_ref, send_sem, recv_sem, local_sem,
):
    experts = lax.axis_size("expert")
    chips = experts // 2
    me = lax.axis_index("expert")
    chip, core = me // 2, me % 2
    outs = (gate_ref, up_ref, down_ref)
    piece_rows = gate_ref.shape[1]
    places = [(chip + k) % chips for k in sorted(range(1, chips), key=lambda k: abs(k - chips // 2))] + [chip]

    barrier = pltpu.get_barrier_semaphore()
    for place in places[:-1]:
        pl.semaphore_signal(barrier, inc=1, device_id={"expert": 2 * place + core}, device_id_type=MESH)
    pl.semaphore_wait(barrier, chips - 1)

    def remote(place, which, landing):
        return pltpu.make_async_remote_copy(
            src_ref=merged_ref.at[place, pl.ds(which * piece_rows, piece_rows)],
            dst_ref=outs[which].at[landing],
            send_sem=send_sem.at[place, which],
            recv_sem=recv_sem.at[landing, which],
            device_id={"expert": 2 * place + core},
            device_id_type=MESH,
        )

    tall = 16
    for place in places:
        for which in range(3):
            def rows(index, carry):
                at = pl.ds(pl.multiple_of(which * piece_rows + index * tall, tall), tall)
                total = jnp.zeros((tall, got_ref.shape[2]), jnp.float32)
                for expert in range(experts):
                    part = jnp.where(place_ref[expert] == place, share_ref[expert, at], 0.0)
                    total = total + got_ref[expert, at].astype(jnp.float32) * part
                merged_ref[place, at] = total.astype(jnp.bfloat16)
                return carry

            lax.fori_loop(0, piece_rows // tall, rows, 0)
            if place is not places[-1]:
                remote(place, which, chip).start()
    keep = [
        pltpu.make_async_copy(
            merged_ref.at[chip, pl.ds(which * piece_rows, piece_rows)], outs[which].at[chip], local_sem.at[which]
        )
        for which in range(3)
    ]
    for copy in keep:
        copy.start()
    for copy in keep:
        copy.wait()
    for place in places[:-1]:
        for which in range(3):
            remote(place, which, chip).wait_send()
            remote(place, which, place).wait_recv()


def deliver(place, share, got):
    experts, rows, half_cols = got.shape
    chips = experts // 2
    vmem = pl.BlockSpec(memory_space=pltpu.VMEM)
    dma = pltpu.SemaphoreType.DMA
    return pl.pallas_call(
        deliver_kernel,
        out_shape=tuple(jax.ShapeDtypeStruct((chips, rows // 3, half_cols), jnp.bfloat16) for _ in range(3)),
        in_specs=[pl.BlockSpec(memory_space=pltpu.SMEM), vmem, vmem],
        out_specs=(pl.BlockSpec(memory_space=pl.ANY),) * 3,
        scratch_shapes=[
            pltpu.VMEM((chips, rows, half_cols), jnp.bfloat16),
            dma((chips, 3)), dma((chips, 3)), dma((3,)),
        ],
        compiler_params=pltpu.CompilerParams(
            collective_id=1, has_side_effects=True, vmem_limit_bytes=40 * 1024 * 1024
        ),
        name="deliver",
    )(place, share, got)


def with_scales(tokens, scales, routes):
    scale_cols = -(-lax.axis_size("expert") // LANES) * LANES
    chosen = routes[:, :, None] == jnp.arange(scale_cols, dtype=jnp.int32)[None, None, :]
    scale_of = jnp.sum(jnp.where(chosen, scales[:, :, None].astype(jnp.float32), 0.0), axis=1)
    return jnp.concatenate([tokens, scale_of.astype(jnp.bfloat16)], axis=1)


def exchange(*weights):
    expert_count = lax.axis_size("expert")
    blocks, (_, hid_dev, model_width) = expert_count // 2, weights[0].shape

    def split(weight):
        return weight[0].reshape(blocks, hid_dev // blocks, 2, model_width // 2).transpose(0, 2, 1, 3)

    sent = jnp.stack([split(w) for w in weights], axis=2)
    sent = sent.reshape(expert_count, 3 * (hid_dev // blocks), model_width // 2)
    return lax.all_to_all(sent, "expert", split_axis=0, concat_axis=0, tiled=True)


def per_device(
    tokens, cotangent, routes, route_weight, gate_weight, up_weight, down_weight, cluster_of, owner
):
    expert_count = lax.axis_size("expert")
    row_count, model_width = tokens.shape
    top_count = routes.shape[1]
    capacity = max(2, row_count * top_count * 9 // (8 * expert_count))
    energy = jnp.mean(jnp.square(cotangent.astype(jnp.float32)), axis=1)
    scales = (jnp.square(route_weight) * energy[:, None]).astype(jnp.bfloat16)
    hid_dev = gate_weight.shape[1]
    half_cols = model_width // 2
    blocks = expert_count // 2
    block_rows = hid_dev // blocks

    dense = row_count <= 2 * capacity and expert_count % 8 == 0 and block_rows % 16 == 0
    if dense:
        extended = with_scales(tokens, scales, routes)
        got, peer_fisher = spread(extended, gate_weight[0], up_weight[0], down_weight[0])
    else:
        got = exchange(gate_weight, up_weight, down_weight)
        peer_fisher = routed_fisher(tokens, scales, routes, gate_weight, up_weight, capacity)
    clusters = owner.shape[0]
    same = (cluster_of[None, :] == cluster_of[:, None]).astype(jnp.float32)
    share_all = peer_fisher / jnp.dot(same, peer_fisher, precision=lax.Precision.HIGHEST)
    my_index = lax.axis_index("expert")
    share = lax.dynamic_slice_in_dim(share_all, my_index, 1, 0)
    window = lax.dynamic_slice_in_dim(share_all, (my_index // 2) * block_rows, block_rows, 1)
    window = jnp.concatenate([window] * 3, axis=1)[:, :, None]
    if dense and clusters == blocks:
        outs = [out.reshape(1, hid_dev, half_cols) for out in deliver(owner[cluster_of], window, got)]
    else:
        merged = merge_blocks(owner[cluster_of], window, got, clusters)
        groups = [list(range(h, expert_count, 2)) for h in range(2)]
        final = lax.all_to_all(
            merged, "expert", split_axis=0, concat_axis=0, tiled=True, axis_index_groups=groups
        ).reshape(blocks, 3, block_rows, half_cols)
        outs = [final[:, i].reshape(1, hid_dev, half_cols) for i in range(3)]
    return (*outs, share)


def solution(mesh):
    return jax.shard_map(
        per_device,
        mesh=mesh,
        in_specs=(
            P(("expert", "dp"), None),
            P(("expert", "dp"), None),
            P(("expert", "dp"), None),
            P(("expert", "dp"), None),
            P("expert", "dp", None),
            P("expert", "dp", None),
            P("expert", "dp", None),
            P(),
            P(),
        ),
        out_specs=(
            P("expert", "dp", None),
            P("expert", "dp", None),
            P("expert", "dp", None),
            P("expert", "dp"),
        ),
        check_vma=False,
    )
```

```python
import functools

import jax
import jax.numpy as jnp
from jax import lax
from jax.experimental import pallas as pl
from jax.experimental.pallas import tpu as pltpu
from jax.sharding import PartitionSpec as P

LANES = 128
MESH = pl.DeviceIdType.MESH


def fused_kernel(
    cluster_ref, owner_ref, routes_ref, route_weight_ref, tokens_ref, cotangent_ref, gate_ref, up_ref, down_ref,
    out_gate_ref, out_up_ref, out_down_ref, share_ref,
    rows_ref, slope_ref, held_ref, parts_ref, others_ref, fisher_ref, all_ref, turned_ref, coef_ref, got_ref,
    merged_ref,
    token_send, token_recv, swap_send, swap_recv, part_send, part_recv, fisher_send, fisher_recv,
    piece_send, piece_recv, out_send, out_recv, own_sem, keep_sem,
    *, factor,
):
    experts, dp_count = lax.axis_size("expert"), lax.axis_size("dp")
    depth, chips = experts // 4, experts // 2
    me, my_dp = lax.axis_index("expert"), lax.axis_index("dp")
    z, y, core = me // 4, (me // 2) % 2, me % 2
    chip = me // 2
    row_count = tokens_ref.shape[0]
    hid_dev, model_width = gate_ref.shape
    half_cols = model_width // 2
    piece_rows = got_ref.shape[2]
    weights = (gate_ref, up_ref, down_ref)
    outs = (out_gate_ref, out_up_ref, out_down_ref)
    half_depth = depth // 2
    far_z, near_z = (1 - z // half_depth) * half_depth, z // half_depth * half_depth
    far_peers = [
        (far_z + (z + dz) % half_depth) * 4 + (me + k) % 4 for k in (0, 2, 1, 3) for dz in range(half_depth)
    ]
    near_peers = [
        (near_z + (z + dz) % half_depth) * 4 + (me + k) % 4 for dz in range(1, half_depth) for k in (0, 2, 1, 3)
    ] + [z * 4 + (me + k) % 4 for k in (2, 1, 3)]
    peers = far_peers + near_peers
    dp_of = [(my_dp + k) % dp_count for k in range(dp_count)]
    across = z * 4 + (1 - y) * 2 + core
    partner = z * 4 + y * 2 + (1 - core)

    def block_of(which, target):
        return weights[which].at[
            pl.ds((target // 2) * piece_rows, piece_rows), pl.ds((target % 2) * half_cols, half_cols)
        ]

    barrier = pltpu.get_barrier_semaphore()
    for peer in peers:
        pl.semaphore_signal(barrier, inc=1, device_id={"expert": peer}, device_id_type=MESH)
    for other in dp_of[1:]:
        pl.semaphore_signal(barrier, inc=1, device_id={"dp": other}, device_id_type=MESH)
    own = [
        pltpu.make_async_copy(gate_ref, held_ref.at[0, 0], own_sem.at[1]),
        pltpu.make_async_copy(up_ref, held_ref.at[0, 1], own_sem.at[2]),
    ] + [
        pltpu.make_async_copy(block_of(which, me), got_ref.at[me, which], own_sem.at[3 + which])
        for which in range(3)
    ]
    first = [
        pltpu.make_async_copy(cotangent_ref, slope_ref, own_sem.at[6]),
        pltpu.make_async_copy(tokens_ref, rows_ref.at[me, :, pl.ds(0, model_width)], own_sem.at[0]),
    ]
    for copy in first + own:
        copy.start()
    first[0].wait()
    slope = slope_ref[...].astype(jnp.float32)
    energy = jnp.sum(slope * slope, axis=1, keepdims=True) / float(model_width)
    energy_row = jnp.transpose(jnp.broadcast_to(energy, (row_count, LANES)))[:routes_ref.shape[0]]
    scale_row = jnp.square(route_weight_ref[...]) * energy_row
    expert_at = lax.broadcasted_iota(jnp.int32, (LANES, row_count), 0)
    scale_of = jnp.zeros((LANES, row_count), jnp.float32)
    for choice in range(routes_ref.shape[0]):
        chosen = routes_ref[choice:choice + 1] == expert_at
        scale_of = scale_of + jnp.where(chosen, scale_row[choice:choice + 1], 0.0)
    rows_ref[me, :, model_width:] = jnp.transpose(scale_of).astype(jnp.bfloat16)
    first[1].wait()
    pl.semaphore_wait(barrier, experts - 1 + dp_count - 1)

    def token_copy(slot, kind, peer, source=None):
        return pltpu.make_async_remote_copy(
            src_ref=rows_ref.at[slot] if source is None else source,
            dst_ref=rows_ref.at[slot],
            send_sem=token_send.at[kind, slot],
            recv_sem=token_recv.at[slot],
            device_id={"expert": peer},
            device_id_type=MESH,
        )

    def own_line(act):
        for sign, kind in ((1, 0), (-1, 1)):
            @pl.when((z + sign >= 0) & (z + sign < depth))
            def _():
                act(token_copy(me, kind, me + 4 * sign), None)
        act(token_copy(me, 2, across), None)
        act(token_copy(me, 3, partner), None)

    def line(act, distance):
        for sign, kind in ((1, 0), (-1, 1)):
            origin = z - sign * distance

            @pl.when((origin >= 0) & (origin < depth))
            def _():
                slot = origin * 4 + y * 2 + core
                act(None, slot)

                @pl.when((z + sign >= 0) & (z + sign < depth))
                def _():
                    act(token_copy(slot, kind, me + 4 * sign), None)
                act(token_copy(slot, 2, across), None)
                act(token_copy(slot, 3, partner), None)

    def beside(act):
        for distance in range(depth):
            for sign in (1, -1) if distance else (1,):
                origin = z - sign * distance

                @pl.when((origin >= 0) & (origin < depth))
                def _():
                    slot = origin * 4 + (1 - y) * 2 + core
                    act(None, slot)
                    act(token_copy(slot, 3, partner), None)

    def begin(copy, slot):
        if copy is None:
            token_copy(slot, 0, partner).wait_recv()
        else:
            copy.start()

    def finish(copy, slot):
        if copy is not None:
            copy.wait_send()

    def swap_copy(shift, which):
        return pltpu.make_async_remote_copy(
            src_ref=weights[which],
            dst_ref=held_ref.at[shift, which],
            send_sem=swap_send.at[shift, which],
            recv_sem=swap_recv.at[shift, which],
            device_id={"dp": dp_of[(dp_count - shift) % dp_count]},
            device_id_type=MESH,
        )

    def piece_copy(which, peer, landing):
        return pltpu.make_async_remote_copy(
            src_ref=block_of(which, peer),
            dst_ref=got_ref.at[landing, which],
            send_sem=piece_send.at[peer, which],
            recv_sem=piece_recv.at[landing, which],
            device_id={"expert": peer},
            device_id_type=MESH,
        )

    def pieces(which, targets):
        for peer in targets:
            piece_copy(which, peer, me).start()

    swaps = [swap_copy(shift, which) for shift in range(1, dp_count) for which in range(2)]
    for copy in swaps:
        copy.start()
    own_line(begin)
    for distance in range(1, depth):
        line(begin, distance)
    pieces(0, far_peers)
    pieces(1, far_peers)
    pieces(2, far_peers)
    for copy in own:
        copy.wait()
    beside(begin)
    for zs in range(depth):
        for ys in range(2):
            token_copy(zs * 4 + ys * 2 + 1 - core, 0, partner).wait_recv()

    for which in range(3):
        pieces(which, near_peers)

    contract = (((1,), (1,)), ((), ()))
    group = 4

    def compute(shift):
        parts_ref[shift] = jnp.zeros_like(parts_ref[shift])

        def step(index, carry):
            block = rows_ref[pl.ds(index * group, group)].reshape(group * row_count, rows_ref.shape[2])
            tokens = block[:, :model_width]
            pre_gate = lax.dot_general(
                tokens, held_ref[shift, 0], contract, preferred_element_type=jnp.float32) * factor
            pre_up = lax.dot_general(
                tokens, held_ref[shift, 1], contract, preferred_element_type=jnp.float32) * factor
            act = pre_gate / (1.0 + jnp.exp(-pre_gate)) * pre_up
            columns = block[:, model_width:].astype(jnp.float32)
            lane = lax.broadcasted_iota(jnp.int32, columns.shape, 1)
            scale = jnp.sum(jnp.where(lane == me, columns, 0.0), axis=1, keepdims=True)
            parts_ref[shift] += jnp.sum(act * act * scale, axis=0, keepdims=True)
            return carry

        lax.fori_loop(0, experts // group, step, 0)

    compute(0)
    for shift in range(1, dp_count):
        for which in range(2):
            swap_copy(shift, which).wait_recv()
        compute(shift)

    def part_copy(shift):
        return pltpu.make_async_remote_copy(
            src_ref=parts_ref.at[shift],
            dst_ref=others_ref.at[shift],
            send_sem=part_send.at[shift],
            recv_sem=part_recv.at[shift],
            device_id={"dp": dp_of[shift]},
            device_id_type=MESH,
        )

    for shift in range(1, dp_count):
        part_copy(shift).start()
    total = parts_ref[0]
    for shift in range(1, dp_count):
        part_copy(shift).wait()
        total = total + others_ref[shift]
    fisher_ref[me] = total

    def fisher_copy(peer, landing):
        return pltpu.make_async_remote_copy(
            src_ref=fisher_ref.at[me],
            dst_ref=fisher_ref.at[landing],
            send_sem=fisher_send.at[peer],
            recv_sem=fisher_recv.at[landing],
            device_id={"expert": peer},
            device_id_type=MESH,
        )

    for peer in peers:
        fisher_copy(peer, me).start()
    all_ref[...] = jnp.zeros_like(all_ref)
    for peer in peers:
        pltpu.make_async_remote_copy(
            src_ref=fisher_ref.at[me], dst_ref=fisher_ref.at[peer], send_sem=fisher_send.at[peer],
            recv_sem=fisher_recv.at[peer], device_id={"expert": peer}, device_id_type=MESH,
        ).wait_recv()

    def same_place(left, right):
        return jnp.where(cluster_ref[left] == cluster_ref[right], 1.0, 0.0)

    lane = lax.broadcasted_iota(jnp.int32, (1, LANES), 1)
    lane_place = jnp.full((1, LANES), -1, jnp.int32)
    for expert in range(experts):
        lane_place = jnp.where(lane == expert, owner_ref[cluster_ref[expert]], lane_place)

    for expert in range(experts):
        total = jnp.zeros((1, hid_dev), jnp.float32)
        for other in range(experts):
            total = total + fisher_ref[other] * same_place(expert, other)
        all_ref[expert:expert + 1] = fisher_ref[expert] / total
    share_ref[...] = all_ref[pl.ds(me, 1)]
    turned_ref[...] = jnp.transpose(all_ref[...])
    window = turned_ref[pl.ds(pl.multiple_of(chip * piece_rows, 16), piece_rows)]
    for place in range(chips):
        coef_ref[place] = jnp.where(lane_place == place, window, 0.0)

    def out_copy(which, place, landing):
        return pltpu.make_async_remote_copy(
            src_ref=merged_ref.at[which, place],
            dst_ref=outs[which].at[landing],
            send_sem=out_send.at[which, place],
            recv_sem=out_recv.at[which, landing],
            device_id={"expert": 2 * place + core},
            device_id_type=MESH,
        )

    tall, wide = 16, 512
    half_chips = chips // 2
    far_places = [far_z * 2 + (chip + k) % half_chips for k in range(half_chips)]
    near_places = [near_z * 2 + (chip + k) % half_chips for k in range(1, half_chips)] + [chip]

    def merge(which, places):
        def rows(index, carry):
            at = pl.ds(pl.multiple_of(index * tall, tall), tall)
            scales = [coef_ref[place, at] for place in places]
            for left in range(0, half_cols, wide):
                sums = [jnp.zeros((tall, wide), jnp.float32) for _ in places]
                for expert in range(experts):
                    block = got_ref[expert, which, at, left:left + wide].astype(jnp.float32)
                    sums = [
                        total + block * scale[:, expert:expert + 1] for total, scale in zip(sums, scales)
                    ]
                for place, total in zip(places, sums):
                    merged_ref[which, place, at, left:left + wide] = total.astype(jnp.bfloat16)
            return carry

        lax.fori_loop(0, piece_rows // tall, rows, 0)
        for place in places:
            if place is not chip:
                out_copy(which, place, chip).start()

    def arrived(which):
        for peer in peers:
            piece_copy(which, peer, peer).wait_recv()

    for which in range(2):
        arrived(which)
        merge(which, far_places)
    for which in range(2):
        merge(which, near_places)
    arrived(2)
    merge(2, far_places)
    merge(2, near_places)
    keep = [
        pltpu.make_async_copy(merged_ref.at[which, chip], outs[which].at[chip], keep_sem.at[which])
        for which in range(3)
    ]
    for copy in keep:
        copy.start()

    own_line(finish)
    for distance in range(1, depth):
        line(finish, distance)
    beside(finish)
    for copy in swaps:
        copy.wait_send()
    for peer in peers:
        fisher_copy(peer, me).wait_send()
        for which in range(3):
            piece_copy(which, peer, me).wait_send()
    for copy in keep:
        copy.wait()
    for which in range(3):
        for place in far_places + near_places[:-1]:
            out_copy(which, place, chip).wait_send()
            out_copy(which, place, place).wait_recv()


def fused(tokens, cotangent, routes, route_weight, gate, up, down, cluster_of, owner):
    experts, dp_count = lax.axis_size("expert"), lax.axis_size("dp")
    row_count, model_width = tokens.shape
    hid_dev, wide = gate.shape[0], model_width + LANES
    chips, half_cols = experts // 2, model_width // 2
    piece_rows = hid_dev // chips
    smem = pl.BlockSpec(memory_space=pltpu.SMEM)
    anywhere = pl.BlockSpec(memory_space=pl.ANY)
    vmem = pl.BlockSpec(memory_space=pltpu.VMEM)
    dma = pltpu.SemaphoreType.DMA
    narrow, full = jnp.bfloat16, jnp.float32
    *outs, share = pl.pallas_call(
        functools.partial(fused_kernel, factor=1.0 / float(model_width) ** 0.5),
        out_shape=tuple(jax.ShapeDtypeStruct((chips, piece_rows, half_cols), narrow) for _ in range(3)) + (
            jax.ShapeDtypeStruct((1, hid_dev), full),),
        in_specs=[smem, smem, vmem, vmem] + [anywhere] * 5,
        out_specs=(anywhere,) * 3 + (vmem,),
        scratch_shapes=[
            pltpu.VMEM((experts, row_count, wide), narrow),
            pltpu.VMEM((row_count, model_width), narrow),
            pltpu.VMEM((dp_count, 2, hid_dev, model_width), narrow),
            pltpu.VMEM((dp_count, 1, hid_dev), full),
            pltpu.VMEM((dp_count, 1, hid_dev), full),
            pltpu.VMEM((experts, 1, hid_dev), full),
            pltpu.VMEM((LANES, hid_dev), full),
            pltpu.VMEM((hid_dev, LANES), full),
            pltpu.VMEM((chips, piece_rows, LANES), full),
            pltpu.VMEM((experts, 3, piece_rows, half_cols), narrow),
            pltpu.VMEM((3, chips, piece_rows, half_cols), narrow),
            dma((4, experts)), dma((experts,)),
            dma((dp_count, 2)), dma((dp_count, 2)),
            dma((dp_count,)), dma((dp_count,)),
            dma((experts,)), dma((experts,)),
            dma((experts, 3)), dma((experts, 3)),
            dma((3, chips)), dma((3, chips)),
            dma((7,)), dma((3,)),
        ],
        compiler_params=pltpu.CompilerParams(
            collective_id=0, has_side_effects=True, vmem_limit_bytes=60 * 1024 * 1024
        ),
        name="fused",
    )(cluster_of, owner, routes.T, route_weight.T, tokens, cotangent, gate, up, down)
    return tuple(out.reshape(1, hid_dev, half_cols) for out in outs) + (share,)


def merge_kernel(place_ref, share_ref, got_ref, out_ref, total_ref):
    total_ref[...] = jnp.zeros_like(total_ref)

    def add(expert, carry):
        place = place_ref[expert]
        weighted = got_ref[expert].astype(jnp.float32) * share_ref[expert]
        total_ref[place] = total_ref[place] + weighted
        return carry

    lax.fori_loop(0, got_ref.shape[0], add, 0)
    out_ref[...] = total_ref[...].astype(jnp.bfloat16)


def merge_blocks(place, share, got, clusters):
    shape = (clusters,) + got.shape[1:]
    return pl.pallas_call(
        merge_kernel,
        out_shape=jax.ShapeDtypeStruct(shape, jnp.bfloat16),
        in_specs=[
            pl.BlockSpec(memory_space=pltpu.SMEM),
            pl.BlockSpec(memory_space=pltpu.VMEM),
            pl.BlockSpec(memory_space=pltpu.VMEM),
        ],
        out_specs=pl.BlockSpec(memory_space=pltpu.VMEM),
        scratch_shapes=[pltpu.VMEM(shape, jnp.float32)],
        cost_estimate=pl.CostEstimate(flops=2 * got.size, bytes_accessed=3 * got.size, transcendentals=0),
        name="merge",
    )(place, share, got)


def routed_fisher(tokens, scales, routes, gate_weight, up_weight, capacity):
    expert_count = lax.axis_size("expert")
    row_count, model_width = tokens.shape
    top_count = routes.shape[1]
    scales = scales.reshape(-1)
    flat_ids = routes.reshape(-1)
    one_hot = (flat_ids[:, None] == jnp.arange(expert_count, dtype=jnp.int32)[None, :]).astype(
        jnp.int32
    )
    rank_ids = jnp.sum((jnp.cumsum(one_hot, axis=0) - one_hot) * one_hot, axis=1)
    slot_ids = flat_ids * capacity + rank_ids
    source = jnp.arange(row_count * top_count, dtype=jnp.int32) // top_count
    send_rows = (
        jnp.zeros((expert_count * capacity, model_width), jnp.bfloat16)
        .at[slot_ids]
        .set(tokens[source])
    )
    send_scales = jnp.zeros((expert_count * capacity,), jnp.bfloat16).at[slot_ids].set(scales)
    recv_rows, recv_scales = (
        lax.all_to_all(
            send_rows.reshape(expert_count, capacity, model_width),
            "expert",
            split_axis=0,
            concat_axis=0,
            tiled=True,
        ),
        lax.all_to_all(
            send_scales.reshape(expert_count, capacity),
            "expert",
            split_axis=0,
            concat_axis=0,
            tiled=True,
        ),
    )
    inputs = recv_rows.reshape(-1, model_width)
    weights_s = recv_scales.reshape(-1).astype(jnp.float32)
    hid_dev = gate_weight.shape[1]
    factor = 1.0 / jnp.sqrt(jnp.float32(model_width))
    pre_gate = (
        jnp.dot(
            inputs,
            lax.all_gather(gate_weight[0], "dp", axis=0, tiled=True).T,
            preferred_element_type=jnp.float32,
        )
        * factor
    )
    pre_up = (
        jnp.dot(
            inputs,
            lax.all_gather(up_weight[0], "dp", axis=0, tiled=True).T,
            preferred_element_type=jnp.float32,
        )
        * factor
    )
    act = jax.nn.silu(pre_gate) * pre_up
    part = jnp.dot(weights_s, act * act, precision=lax.Precision.HIGHEST)
    whole_sum = lax.psum(part, "dp")
    own_fisher = lax.dynamic_slice_in_dim(whole_sum, lax.axis_index("dp") * hid_dev, hid_dev)
    return lax.all_gather(own_fisher[None, :], "expert", axis=0, tiled=True)


def exchange(*weights):
    expert_count = lax.axis_size("expert")
    blocks, (_, hid_dev, model_width) = expert_count // 2, weights[0].shape

    def split(weight):
        return weight[0].reshape(blocks, hid_dev // blocks, 2, model_width // 2).transpose(0, 2, 1, 3)

    sent = jnp.stack([split(w) for w in weights], axis=2)
    sent = sent.reshape(expert_count, 3 * (hid_dev // blocks), model_width // 2)
    return lax.all_to_all(sent, "expert", split_axis=0, concat_axis=0, tiled=True)


def per_device(
    tokens, cotangent, routes, route_weight, gate_weight, up_weight, down_weight, cluster_of, owner
):
    expert_count = lax.axis_size("expert")
    row_count, model_width = tokens.shape
    top_count = routes.shape[1]
    capacity = max(2, row_count * top_count * 9 // (8 * expert_count))
    hid_dev = gate_weight.shape[1]
    half_cols = model_width // 2
    blocks = expert_count // 2
    block_rows = hid_dev // blocks

    dense = row_count <= 2 * capacity and expert_count % 8 == 0 and block_rows % 16 == 0
    tiled = row_count % LANES == 0 and expert_count <= LANES
    clusters = owner.shape[0]
    if dense and tiled and clusters == blocks:
        return fused(
            tokens, cotangent, routes, route_weight, gate_weight[0], up_weight[0], down_weight[0], cluster_of, owner)
    place = owner[cluster_of]
    energy = jnp.mean(jnp.square(cotangent.astype(jnp.float32)), axis=1)
    scales = (jnp.square(route_weight) * energy[:, None]).astype(jnp.bfloat16)
    got = exchange(gate_weight, up_weight, down_weight)
    peer_fisher = routed_fisher(tokens, scales, routes, gate_weight, up_weight, capacity)
    same = (cluster_of[None, :] == cluster_of[:, None]).astype(jnp.float32)
    share_all = peer_fisher / jnp.dot(same, peer_fisher, precision=lax.Precision.HIGHEST)
    my_index = lax.axis_index("expert")
    share = lax.dynamic_slice_in_dim(share_all, my_index, 1, 0)
    window = lax.dynamic_slice_in_dim(share_all, (my_index // 2) * block_rows, block_rows, 1)
    window = jnp.concatenate([window] * 3, axis=1)[:, :, None]
    merged = merge_blocks(place, window, got, clusters)
    groups = [list(range(h, expert_count, 2)) for h in range(2)]
    final = lax.all_to_all(
        merged, "expert", split_axis=0, concat_axis=0, tiled=True, axis_index_groups=groups
    ).reshape(blocks, 3, block_rows, half_cols)
    outs = [final[:, i].reshape(1, hid_dev, half_cols) for i in range(3)]
    return (*outs, share)


def solution(mesh):
    return jax.shard_map(
        per_device,
        mesh=mesh,
        in_specs=(
            P(("expert", "dp"), None),
            P(("expert", "dp"), None),
            P(("expert", "dp"), None),
            P(("expert", "dp"), None),
            P("expert", "dp", None),
            P("expert", "dp", None),
            P("expert", "dp", None),
            P(),
            P(),
        ),
        out_specs=(
            P("expert", "dp", None),
            P("expert", "dp", None),
            P("expert", "dp", None),
            P("expert", "dp"),
        ),
        check_vma=False,
    )
```
